32 devices in a mesh: chan: 8 (over y, x, core), slab: 4 (over z).
Axes of the slice: x: 2, y: 2, z: 4, core: 2. Of those that a mesh axis runs over, the one named last changes fastest.
Arguments:
- activations: bfloat16 [128, 8, 8, 128], P('chan', 'slab'), may hold values from -6 to 6
- cotangent: bfloat16 [128, 8, 8, 128], P('chan', 'slab'), may hold values from -6 to 6
- relu_mask: int32 [128, 8, 8, 128], P('chan', 'slab'), may hold values 0 or 1
- weights: bfloat16 [3, 3, 3, 128, 128], replicated, may hold values from -0.109375 to 0.109375
Outputs:
- pre: bfloat16 [128, 8, 8, 128], P('chan', 'slab')
- grad_input: bfloat16 [128, 8, 8, 128], P('chan', 'slab')
The draws below stay inside these ranges and needn't reach their ends.
All inputs are finite; a program needn't handle non-finite values. No bound on the sum of `relu_mask` on one device may be relied on, other than what follows from the above.
Results may differ from the reference program's by a relative error of at most 0.0013.
Values may be sent and summed in bfloat16 or wider, within the bound.
No kernel may reach another device: no remote copies, remote signals or barrier semaphores. Data moves between devices by JAX's collectives and lax.ppermute only.
A program may use at most 64 MiB of HBM per device.

```python
import jax
import jax.numpy as jnp
from jax import lax

CHANNELS = 128
ROWS = 8
COLS = 128
DEPTH = 8


def place_ends(result, rng, smallest, top_value):
    place = [jax.random.randint(jax.random.fold_in(rng, axis), (), 0, length) for axis, length in enumerate(result.shape)]
    longest = result.shape.index(max(result.shape))
    beside = place[:longest] + [(place[longest] + 1) % result.shape[longest]] + place[longest + 1:]
    return result.at[tuple(place)].set(smallest).at[tuple(beside)].set(top_value)


def level_of(stream_key, dims, shards, low, largest):
    factor_of = 1.0
    for axis_at, blocks in shards:
        draws = jax.random.uniform(jax.random.fold_in(jax.random.fold_in(stream_key, 6), axis_at), (blocks,), jnp.float32, low / len(shards), largest / len(shards))
        factor_of = factor_of * jnp.repeat(jnp.exp(draws), dims[axis_at] // blocks).reshape((-1,) + (1,) * (len(dims) - 1 - axis_at))
    return factor_of


def bell_draw(rng, extent, deviation, limit, split=(), dtype=jnp.bfloat16):
    entries = jax.random.normal(rng, extent, jnp.float32) * deviation
    if len(split) > 0:
        entries = level_of(rng, extent, split, -0.22, 0.18) * entries
    return jnp.clip(entries, min=-limit, max=limit).astype(dtype)


def setup_inputs(seed: int = 0) -> dict:
    key_of = jax.random.split(jax.random.key(seed), 5)
    activations = bell_draw(key_of[0], (CHANNELS, DEPTH, ROWS, COLS), 1.0, 6.0, ((0, 8), (1, 4)))
    cotangent = bell_draw(key_of[1], (CHANNELS, DEPTH, ROWS, COLS), 1.0, 6.0, ((0, 8), (1, 4)))
    relu_mask = place_ends((jax.random.randint(key_of[2], (CHANNELS, DEPTH, ROWS, COLS), 0, 2) < 1).astype(jnp.int32), jax.random.fold_in(key_of[2], 1), 0, 1)
    weights = bell_draw(key_of[3], (3, 3, 3, CHANNELS, CHANNELS), (27 * CHANNELS) ** -0.5, 0.109375)
    return {"activations": activations, "cotangent": cotangent, "relu_mask": relu_mask, "weights": weights}


def convolve(inputs, kernel):
    return lax.conv_general_dilated(inputs, kernel, (1, 1, 1), ((1, 1), (1, 1), (1, 1)), dimension_numbers=('NCDHW', 'DHWOI', 'NCDHW'), precision=lax.Precision.HIGHEST)

def reference(activations, cotangent, relu_mask, weights):
    inputs = activations.astype(jnp.float32)[None]
    kernel = weights.astype(jnp.float32)
    pre = convolve(inputs, kernel)[0].astype(jnp.bfloat16)
    masked = jnp.where(relu_mask == 1, cotangent, jnp.zeros_like(cotangent))
    _, pullback = jax.vjp(lambda value: convolve(value, kernel), inputs)
    grad_input = pullback(masked.astype(jnp.float32)[None])[0][0].astype(jnp.bfloat16)
    return (pre, grad_input)
```

```python
import functools

import jax
import jax.numpy as jnp
from jax import lax
from jax.experimental import pallas as pl
from jax.experimental.pallas import tpu as pltpu
from jax.sharding import PartitionSpec as P

LANES = 128
TILE = 16
F32 = jnp.float32


def with_halo(shard, sides, width):
    for axis, dim in sides:
        devices, length = (lax.axis_size(axis), shard.shape[dim])
        up = [(i, (i + 1) % devices) for i in range(devices - 1)]
        down = [(j, i) for i, j in up]
        last = lax.slice_in_dim(shard, length - width, length, axis=dim)
        first = lax.slice_in_dim(shard, 0, width, axis=dim)
        before = lax.ppermute(last, axis, up)
        after = lax.ppermute(first, axis, down)
        shard = jnp.concatenate([before, shard, after], axis=dim)
    return shard


def tap_sum(weights, padded, planes, height, breadth, equation, flipped):
    total = None
    for i in range(3):
        for j in range(3):
            for k in range(3):
                a, b, c = (2 - i, 2 - j, 2 - k) if flipped else (i, j, k)
                window = padded[:, a : a + planes, b : b + height, c : c + breadth]
                term = jnp.einsum(equation, weights[i, j, k], window, preferred_element_type=F32)
                total = term if total is None else total + term
    return total.astype(jnp.bfloat16)


def general_body(activations, cotangent, relu_mask, weights):
    planes, breadth = activations.shape[1], activations.shape[3]
    masked = jnp.where(relu_mask == 1, cotangent, jnp.zeros_like(cotangent))
    stacked = jnp.stack([activations, masked])
    patches = lax.all_to_all(stacked, "chan", split_axis=3, concat_axis=1, tiled=True)
    rimmed = with_halo(patches, (("chan", 3), ("slab", 2)), 1)
    padded = jnp.pad(rimmed, ((0, 0), (0, 0), (0, 0), (0, 0), (1, 1)))
    height = patches.shape[3]
    pre = tap_sum(weights, padded[0], planes, height, breadth, "oi,idhw->odhw", False)
    grad = tap_sum(weights, padded[1], planes, height, breadth, "oi,odhw->idhw", True)
    return tuple(
        lax.all_to_all(block, "chan", split_axis=0, concat_axis=2, tiled=True) for block in (pre, grad)
    )


def conv_kernel(width, sources, *refs):
    count = len(sources)
    blocks, lhs_ref = refs[:count], refs[count]
    even_ref, odd_ref, inner_ref, x_ref = refs[count + 1 :]
    arrays, rows, planes, _, cols = inner_ref.shape
    me = lax.axis_index("chan")
    even = lax.rem(lax.axis_index("slab"), 2) == 0
    channels = x_ref.shape[2]

    zero = jnp.zeros((channels, planes * cols), jnp.bfloat16)
    for a in range(arrays):
        x_ref[a, 0] = zero
        x_ref[a, rows + 1] = zero
    for block, source in zip(blocks, sources):
        where = pl.ds(pl.multiple_of(jnp.bitwise_xor(me, source) * width, width), width)
        for a in range(arrays):
            for r in range(rows):
                for p in range(planes):
                    x_ref[a, r + 1, where, p * cols : (p + 1) * cols] = block[a, r, p]

    lane = lax.broadcasted_iota(jnp.int32, (width, cols), 1)
    first, last = lane == 0, lane == cols - 1

    def columns(left, mid, right):
        left = jnp.where(first, 0.0, pltpu.roll(left, 1, 1))
        right = jnp.where(last, 0.0, pltpu.roll(right, cols - 1, 1))
        return left + mid + right

    for a in range(arrays):
        lhs = lhs_ref[a]
        for r in range(rows):
            window = x_ref[a, r : r + 3].reshape(3 * channels, planes * cols)
            y = jnp.dot(lhs, window, preferred_element_type=F32)

            def part(t, k, p):
                top = (t * 3 + k) * width
                return y[top : top + width, p * cols : (p + 1) * cols]

            outs = {}
            for q in range(-1, planes + 1):
                taps = [
                    functools.reduce(
                        lambda u, v: u + v,
                        [part(p - q + 1, k, p) for p in range(planes) if 0 <= p - q + 1 <= 2],
                    )
                    for k in range(3)
                ]
                outs[q] = columns(*taps)
            even_ref[a, r] = jnp.where(even, outs[planes], outs[-1])
            odd_ref[a, r] = jnp.where(even, outs[-1], outs[planes])
            for p in range(planes):
                inner_ref[a, r, p] = outs[p]


def add_kernel(inner_ref, even_ref, odd_ref, pre_ref, grad_ref, turned_ref):
    arrays, rows, planes, width, cols = inner_ref.shape
    even = lax.rem(lax.axis_index("slab"), 2) == 0
    for a, out_ref in enumerate((pre_ref, grad_ref)):
        for p in range(planes):
            for r in range(rows):
                value = inner_ref[a, r, p]
                if p == 0:
                    value = value + jnp.where(even, odd_ref[a, r], even_ref[a, r])
                if p == planes - 1:
                    value = value + jnp.where(even, even_ref[a, r], odd_ref[a, r])
                turned_ref[pl.ds(r, width, stride=rows), :] = value
            out_ref[:, p] = turned_ref[...].reshape(width, rows, cols).astype(jnp.bfloat16)


def aligned_body(activations, cotangent, relu_mask, weights):
    width, planes, rows, cols = activations.shape
    devices, slabs = lax.axis_size("chan"), lax.axis_size("slab")
    channels = width * devices
    masked = jnp.where(relu_mask == 1, cotangent, jnp.zeros_like(cotangent))
    own = jnp.stack([activations, masked]).transpose(0, 3, 2, 1, 4)

    def swap(value, bit):
        return lax.ppermute(value, "chan", [(i, i ^ bit) for i in range(devices)])

    far = list(range(2, devices, 2))
    near = [own] + [swap(own, bit) for bit in far]
    other = swap(jnp.stack(near), 1)
    sources = [0] + far + [1] + [bit + 1 for bit in far]
    blocks = near + [other[i] for i in range(len(near))]

    start = lax.axis_index("chan") * width
    forward = lax.dynamic_slice_in_dim(weights, start, width, 3)
    backward = lax.dynamic_slice_in_dim(weights, start, width, 4)[::-1, ::-1, ::-1].swapaxes(3, 4)
    lhs = jnp.stack([forward, backward]).transpose(0, 1, 3, 4, 2, 5)
    lhs = lhs.reshape(2, 9 * width, 3 * channels)

    edge = jax.ShapeDtypeStruct((2, rows, width, cols), F32)
    even, odd, inner = pl.pallas_call(
        functools.partial(conv_kernel, width, sources),
        out_shape=(edge, edge, jax.ShapeDtypeStruct((2, rows, planes, width, cols), F32)),
        in_specs=[pl.BlockSpec(memory_space=pltpu.VMEM)] * (len(blocks) + 1),
        out_specs=[pl.BlockSpec(memory_space=pltpu.VMEM)] * 3,
        scratch_shapes=[pltpu.VMEM((2, rows + 2, channels, planes * cols), jnp.bfloat16)],
        name="conv",
    )(*blocks, lhs)

    evens = [(i, i + 1) for i in range(0, slabs - 1, 2)]
    odds = [(i, i + 1) for i in range(1, slabs - 1, 2)]
    even, odd = (
        lax.ppermute(v, "slab", pairs + [(j, i) for i, j in pairs]) for v, pairs in ((even, evens), (odd, odds))
    )
    out = jax.ShapeDtypeStruct(activations.shape, jnp.bfloat16)
    return tuple(
        pl.pallas_call(
            add_kernel,
            out_shape=(out, out),
            in_specs=[pl.BlockSpec(memory_space=pltpu.VMEM)] * 3,
            out_specs=[pl.BlockSpec(memory_space=pltpu.VMEM)] * 2,
            scratch_shapes=[pltpu.VMEM((width * rows, cols), F32)],
            name="add",
        )(inner, even, odd)
    )


def body(activations, cotangent, relu_mask, weights):
    width, planes, rows, cols = activations.shape
    devices = lax.axis_size("chan")
    aligned = (
        width % TILE == 0
        and cols == LANES
        and devices & (devices - 1) == 0
        and devices > 1
        and planes >= 2
        and rows % 8 == 0
        and lax.axis_size("slab") > 1
    )
    return (aligned_body if aligned else general_body)(activations, cotangent, relu_mask, weights)


def solution(mesh):
    placed = P("chan", "slab", None, None)
    return jax.shard_map(
        body,
        mesh=mesh,
        in_specs=(placed, placed, placed, P()),
        out_specs=(placed, placed),
        check_vma=False,
    )
```

```python
import functools

import jax
import jax.numpy as jnp
from jax import lax
from jax.experimental import pallas as pl
from jax.experimental.pallas import tpu as pltpu
from jax.sharding import PartitionSpec as P

LANES = 128
TILE = 16
CONV_VMEM, ADD_VMEM = 8 << 20, 4 << 20
F32 = jnp.float32


def with_halo(shard, sides, width):
    for axis, dim in sides:
        devices, length = (lax.axis_size(axis), shard.shape[dim])
        up = [(i, (i + 1) % devices) for i in range(devices - 1)]
        down = [(j, i) for i, j in up]
        last = lax.slice_in_dim(shard, length - width, length, axis=dim)
        first = lax.slice_in_dim(shard, 0, width, axis=dim)
        before = lax.ppermute(last, axis, up)
        after = lax.ppermute(first, axis, down)
        shard = jnp.concatenate([before, shard, after], axis=dim)
    return shard


def tap_sum(weights, padded, planes, height, breadth, equation, flipped):
    total = None
    for i in range(3):
        for j in range(3):
            for k in range(3):
                a, b, c = (2 - i, 2 - j, 2 - k) if flipped else (i, j, k)
                window = padded[:, a : a + planes, b : b + height, c : c + breadth]
                term = jnp.einsum(equation, weights[i, j, k], window, preferred_element_type=F32)
                total = term if total is None else total + term
    return total.astype(jnp.bfloat16)


def general_body(activations, cotangent, relu_mask, weights):
    planes, breadth = activations.shape[1], activations.shape[3]
    masked = jnp.where(relu_mask == 1, cotangent, jnp.zeros_like(cotangent))
    stacked = jnp.stack([activations, masked])
    patches = lax.all_to_all(stacked, "chan", split_axis=3, concat_axis=1, tiled=True)
    rimmed = with_halo(patches, (("chan", 3), ("slab", 2)), 1)
    padded = jnp.pad(rimmed, ((0, 0), (0, 0), (0, 0), (0, 0), (1, 1)))
    height = patches.shape[3]
    pre = tap_sum(weights, padded[0], planes, height, breadth, "oi,idhw->odhw", False)
    grad = tap_sum(weights, padded[1], planes, height, breadth, "oi,odhw->idhw", True)
    return tuple(
        lax.all_to_all(block, "chan", split_axis=0, concat_axis=2, tiled=True) for block in (pre, grad)
    )


def conv_kernel(width, sources, *refs):
    count = len(sources)
    blocks, lhs_ref = refs[:count], refs[count]
    even_ref, odd_ref, inner_ref, x_ref = refs[count + 1 :]
    arrays, rows, planes, _, cols = inner_ref.shape
    me = lax.axis_index("chan")
    even = lax.rem(lax.axis_index("slab"), 2) == 0
    channels = x_ref.shape[2]

    zero = jnp.zeros((channels, planes * cols), jnp.bfloat16)
    for a in range(arrays):
        x_ref[a, 0] = zero
        x_ref[a, rows + 1] = zero
    for block, source in zip(blocks, sources):
        where = pl.ds(pl.multiple_of(jnp.bitwise_xor(me, source) * width, width), width)
        for a in range(arrays):
            for r in range(rows):
                for p in range(planes):
                    x_ref[a, r + 1, where, p * cols : (p + 1) * cols] = block[a, r, p]

    lane = lax.broadcasted_iota(jnp.int32, (width, cols), 1)
    first, last = lane == 0, lane == cols - 1

    def columns(left, mid, right):
        left = jnp.where(first, 0.0, pltpu.roll(left, 1, 1))
        right = jnp.where(last, 0.0, pltpu.roll(right, cols - 1, 1))
        return left + mid + right

    for a in range(arrays):
        lhs = lhs_ref[a]
        for r in range(rows):
            window = x_ref[a, r : r + 3].reshape(3 * channels, planes * cols)
            y = jnp.dot(lhs, window, preferred_element_type=F32)

            def part(t, k, p):
                top = (t * 3 + k) * width
                return y[top : top + width, p * cols : (p + 1) * cols]

            outs = {}
            for q in range(-1, planes + 1):
                taps = [
                    functools.reduce(
                        lambda u, v: u + v,
                        [part(p - q + 1, k, p) for p in range(planes) if 0 <= p - q + 1 <= 2],
                    )
                    for k in range(3)
                ]
                outs[q] = columns(*taps)
            even_ref[a, r] = jnp.where(even, outs[planes], outs[-1])
            odd_ref[a, r] = jnp.where(even, outs[-1], outs[planes])
            for p in range(planes):
                inner_ref[a, r, p] = outs[p]


def add_kernel(inner_ref, even_ref, odd_ref, pre_ref, grad_ref, turned_ref):
    arrays, rows, planes, width, cols = inner_ref.shape
    even = lax.rem(lax.axis_index("slab"), 2) == 0
    for a, out_ref in enumerate((pre_ref, grad_ref)):
        for p in range(planes):
            for r in range(rows):
                value = inner_ref[a, r, p]
                if p == 0:
                    value = value + jnp.where(even, odd_ref[a, r], even_ref[a, r])
                if p == planes - 1:
                    value = value + jnp.where(even, even_ref[a, r], odd_ref[a, r])
                turned_ref[pl.ds(r, width, stride=rows), :] = value
            out_ref[:, p] = turned_ref[...].reshape(width, rows, cols).astype(jnp.bfloat16)


def aligned_body(activations, cotangent, relu_mask, weights):
    width, planes, rows, cols = activations.shape
    devices, slabs = lax.axis_size("chan"), lax.axis_size("slab")
    channels = width * devices
    masked = jnp.where(relu_mask == 1, cotangent, jnp.zeros_like(cotangent))
    own = jnp.stack([activations, masked]).transpose(0, 3, 2, 1, 4)

    def swap(value, bit):
        return lax.ppermute(value, "chan", [(i, i ^ bit) for i in range(devices)])

    far = list(range(2, devices, 2))
    near = [own] + [swap(own, bit) for bit in far]
    sources = [0] + far + [1] + [bit + 1 for bit in far]

    start = lax.axis_index("chan") * width
    forward = lax.dynamic_slice_in_dim(weights, start, width, 3)
    backward = lax.dynamic_slice_in_dim(weights, start, width, 4)[::-1, ::-1, ::-1].swapaxes(3, 4)
    lhs = jnp.stack([forward, backward]).transpose(0, 1, 3, 4, 2, 5)
    lhs = lhs.reshape(2, 9 * width, 3 * channels)

    near[-1], lhs = lax.optimization_barrier((near[-1], lhs))
    blocks = near + [swap(value, 1) for value in near]

    edge = jax.ShapeDtypeStruct((2, rows, width, cols), F32)
    even, odd, inner = pl.pallas_call(
        functools.partial(conv_kernel, width, sources),
        out_shape=(edge, edge, jax.ShapeDtypeStruct((2, rows, planes, width, cols), F32)),
        in_specs=[pl.BlockSpec(memory_space=pltpu.VMEM)] * (len(blocks) + 1),
        out_specs=[pl.BlockSpec(memory_space=pltpu.VMEM)] * 3,
        scratch_shapes=[pltpu.VMEM((2, rows + 2, channels, planes * cols), jnp.bfloat16)],
        compiler_params=pltpu.CompilerParams(vmem_limit_bytes=CONV_VMEM),
        name="conv",
    )(*blocks, lhs)

    evens = [(i, i + 1) for i in range(0, slabs - 1, 2)]
    odds = [(i, i + 1) for i in range(1, slabs - 1, 2)]
    even, odd = (
        lax.ppermute(v, "slab", pairs + [(j, i) for i, j in pairs]) for v, pairs in ((even, evens), (odd, odds))
    )
    out = jax.ShapeDtypeStruct(activations.shape, jnp.bfloat16)
    return tuple(
        pl.pallas_call(
            add_kernel,
            out_shape=(out, out),
            in_specs=[pl.BlockSpec(memory_space=pltpu.VMEM)] * 3,
            out_specs=[pl.BlockSpec(memory_space=pltpu.VMEM)] * 2,
            scratch_shapes=[pltpu.VMEM((width * rows, cols), F32)],
            compiler_params=pltpu.CompilerParams(vmem_limit_bytes=ADD_VMEM),
            name="add",
        )(inner, even, odd)
    )


def body(activations, cotangent, relu_mask, weights):
    width, planes, rows, cols = activations.shape
    devices = lax.axis_size("chan")
    aligned = (
        width % TILE == 0
        and cols == LANES
        and devices & (devices - 1) == 0
        and devices > 1
        and planes >= 2
        and rows % 8 == 0
        and lax.axis_size("slab") > 1
    )
    return (aligned_body if aligned else general_body)(activations, cotangent, relu_mask, weights)


def solution(mesh):
    placed = P("chan", "slab", None, None)
    return jax.shard_map(
        body,
        mesh=mesh,
        in_specs=(placed, placed, placed, P()),
        out_specs=(placed, placed),
        check_vma=False,
    )
```

```python
import functools
import math

import jax
import jax.numpy as jnp
from jax import lax
from jax.experimental import pallas as pl
from jax.experimental.pallas import tpu as pltpu
from jax.sharding import PartitionSpec as P


LANES = 128
TILE = 16
INPUT_MAX, WEIGHT_MAX = 6.0, 0.109375
CONV_VMEM, ADD_VMEM = 8 << 20, 4 << 20
F32 = jnp.float32


def with_halo(shard, sides, width):
    for axis, dim in sides:
        devices, length = (lax.axis_size(axis), shard.shape[dim])
        up = [(i, (i + 1) % devices) for i in range(devices - 1)]
        down = [(j, i) for i, j in up]
        last = lax.slice_in_dim(shard, length - width, length, axis=dim)
        first = lax.slice_in_dim(shard, 0, width, axis=dim)
        before = lax.ppermute(last, axis, up)
        after = lax.ppermute(first, axis, down)
        shard = jnp.concatenate([before, shard, after], axis=dim)
    return shard


def tap_sum(weights, padded, planes, height, breadth, equation, flipped):
    total = None
    for i in range(3):
        for j in range(3):
            for k in range(3):
                a, b, c = (2 - i, 2 - j, 2 - k) if flipped else (i, j, k)
                window = padded[:, a : a + planes, b : b + height, c : c + breadth]
                term = jnp.einsum(equation, weights[i, j, k], window, preferred_element_type=F32)
                total = term if total is None else total + term
    return total.astype(jnp.bfloat16)


def general_body(activations, cotangent, relu_mask, weights):
    planes, breadth = activations.shape[1], activations.shape[3]
    masked = jnp.where(relu_mask == 1, cotangent, jnp.zeros_like(cotangent))
    stacked = jnp.stack([activations, masked])
    patches = lax.all_to_all(stacked, "chan", split_axis=3, concat_axis=1, tiled=True)
    rimmed = with_halo(patches, (("chan", 3), ("slab", 2)), 1)
    padded = jnp.pad(rimmed, ((0, 0), (0, 0), (0, 0), (0, 0), (1, 1)))
    height = patches.shape[3]
    pre = tap_sum(weights, padded[0], planes, height, breadth, "oi,idhw->odhw", False)
    grad = tap_sum(weights, padded[1], planes, height, breadth, "oi,odhw->idhw", True)
    return tuple(
        lax.all_to_all(block, "chan", split_axis=0, concat_axis=2, tiled=True) for block in (pre, grad)
    )


def conv_kernel(width, sources, *refs):
    count = len(sources)
    blocks, lhs_ref = refs[:count], refs[count]
    even_ref, odd_ref, inner_ref, x_ref = refs[count + 1 :]
    arrays, rows, planes, _, cols = inner_ref.shape
    me = lax.axis_index("chan")
    even = lax.rem(lax.axis_index("slab"), 2) == 0
    channels = x_ref.shape[2]

    zero = jnp.zeros((channels, planes * cols), jnp.bfloat16)
    for a in range(arrays):
        x_ref[a, 0] = zero
        x_ref[a, rows + 1] = zero
    for block, source in zip(blocks, sources):
        where = pl.ds(pl.multiple_of(jnp.bitwise_xor(me, source) * width, width), width)
        for a in range(arrays):
            for r in range(rows):
                for p in range(planes):
                    x_ref[a, r + 1, where, p * cols : (p + 1) * cols] = block[a, r, p]

    lane = lax.broadcasted_iota(jnp.int32, (width, cols), 1)
    first, last = lane == 0, lane == cols - 1

    def columns(left, mid, right):
        left = jnp.where(first, 0.0, pltpu.roll(left, 1, 1))
        right = jnp.where(last, 0.0, pltpu.roll(right, cols - 1, 1))
        return left + mid + right

    for a in range(arrays):
        lhs = lhs_ref[a]
        for r in range(rows):
            window = x_ref[a, r : r + 3].reshape(3 * channels, planes * cols)
            y = jnp.dot(lhs, window, preferred_element_type=F32)

            def part(t, k, p):
                top = (t * 3 + k) * width
                return y[top : top + width, p * cols : (p + 1) * cols]

            outs = {}
            for q in range(-1, planes + 1):
                taps = [
                    functools.reduce(
                        lambda u, v: u + v,
                        [part(p - q + 1, k, p) for p in range(planes) if 0 <= p - q + 1 <= 2],
                    )
                    for k in range(3)
                ]
                outs[q] = columns(*taps)
            even_ref[a, r] = jnp.where(even, outs[planes], outs[-1])
            odd_ref[a, r] = jnp.where(even, outs[-1], outs[planes])
            for p in range(planes):
                inner_ref[a, r, p] = outs[p]


def add_kernel(inner_ref, even_ref, odd_ref, pre_ref, grad_ref, turned_ref):
    _, rows, planes, width, cols = inner_ref.shape
    slab = lax.axis_index("slab")
    even = lax.rem(slab, 2) == 0
    below, above = slab > 0, slab < lax.axis_size("slab") - 1
    for a, out_ref in enumerate((pre_ref, grad_ref)):
        for p in range(planes):
            for r in range(rows):
                value = inner_ref[a, r, p]
                if p == 0:
                    value = value + jnp.where(below, jnp.where(even, odd_ref[a, r], even_ref[a, r]), 0.0)
                if p == planes - 1:
                    value = value + jnp.where(above, jnp.where(even, even_ref[a, r], odd_ref[a, r]), 0.0)
                turned_ref[pl.ds(r, width, stride=rows), :] = value
            out_ref[:, p] = turned_ref[...].reshape(width, rows, cols).astype(jnp.bfloat16)


def aligned_body(activations, cotangent, relu_mask, weights):
    width, planes, rows, cols = activations.shape
    devices, slabs = lax.axis_size("chan"), lax.axis_size("slab")
    channels = width * devices
    masked = jnp.where(relu_mask == 1, cotangent, jnp.zeros_like(cotangent))
    own = jnp.stack([activations, masked]).transpose(0, 3, 2, 1, 4)

    def swap(value, bit):
        return lax.ppermute(value, "chan", [(i, i ^ bit) for i in range(devices)])

    far = list(range(2, devices, 2))
    near = [own] + [swap(own, bit) for bit in far]
    sources = [0] + far + [1] + [bit + 1 for bit in far]

    start = lax.axis_index("chan") * width
    forward = lax.dynamic_slice_in_dim(weights, start, width, 3)
    backward = lax.dynamic_slice_in_dim(weights, start, width, 4)[::-1, ::-1, ::-1].swapaxes(3, 4)
    lhs = jnp.stack([forward, backward]).transpose(0, 1, 3, 4, 2, 5)
    lhs = lhs.reshape(2, 9 * width, 3 * channels)

    near[-1], lhs = lax.optimization_barrier((near[-1], lhs))
    blocks = near + [swap(value, 1) for value in near]

    edge = jax.ShapeDtypeStruct((2, rows, width, cols), F32)
    even, odd, inner = pl.pallas_call(
        functools.partial(conv_kernel, width, sources),
        out_shape=(edge, edge, jax.ShapeDtypeStruct((2, rows, planes, width, cols), F32)),
        in_specs=[pl.BlockSpec(memory_space=pltpu.VMEM)] * (len(blocks) + 1),
        out_specs=[pl.BlockSpec(memory_space=pltpu.VMEM)] * 3,
        scratch_shapes=[pltpu.VMEM((2, rows + 2, channels, planes * cols), jnp.bfloat16)],
        compiler_params=pltpu.CompilerParams(vmem_limit_bytes=CONV_VMEM),
        name="conv",
    )(*blocks, lhs)

    largest = 9 * channels * INPUT_MAX * WEIGHT_MAX
    scale = 2.0 ** math.floor(math.log2(float(jnp.finfo(jnp.float16).max) / largest))

    def exchange(value, first):
        partner = {}
        for i in range(first, slabs - 1, 2):
            partner[i], partner[i + 1] = i + 1, i
        pairs = [
            (c * slabs + s, c * slabs + partner[s] if s in partner else (c ^ 1) * slabs + s)
            for c in range(devices)
            for s in range(slabs)
        ]
        value = (value * scale).astype(jnp.float16)
        value = lax.ppermute(value, ("chan", "slab"), pairs)
        return value.astype(F32) * (1 / scale)

    even, odd = exchange(even, 0), exchange(odd, 1)
    out = jax.ShapeDtypeStruct(activations.shape, jnp.bfloat16)
    return tuple(
        pl.pallas_call(
            add_kernel,
            out_shape=(out, out),
            in_specs=[pl.BlockSpec(memory_space=pltpu.VMEM)] * 3,
            out_specs=[pl.BlockSpec(memory_space=pltpu.VMEM)] * 2,
            scratch_shapes=[pltpu.VMEM((width * rows, cols), F32)],
            compiler_params=pltpu.CompilerParams(vmem_limit_bytes=ADD_VMEM),
            name="add",
        )(inner, even, odd)
    )


def body(activations, cotangent, relu_mask, weights):
    width, planes, rows, cols = activations.shape
    devices = lax.axis_size("chan")
    aligned = (
        width % TILE == 0
        and cols == LANES
        and devices & (devices - 1) == 0
        and devices > 1
        and planes >= 2
        and rows % 8 == 0
        and lax.axis_size("slab") > 1
    )
    if not aligned:
        return general_body(activations, cotangent, relu_mask, weights)
    return aligned_body(activations, cotangent, relu_mask, weights)


def solution(mesh):
    placed = P("chan", "slab", None, None)
    return jax.shard_map(
        body,
        mesh=mesh,
        in_specs=(placed, placed, placed, P()),
        out_specs=(placed, placed),
        check_vma=False,
    )
```

```python
import functools
import math

import jax
import jax.numpy as jnp
from jax import lax
from jax.experimental import pallas as pl
from jax.experimental.pallas import tpu as pltpu
from jax.sharding import PartitionSpec as P


LANES = 128
TILE = 16
INPUT_MAX, WEIGHT_MAX = 6.0, 0.109375
CONV_VMEM, ADD_VMEM = 8 << 20, 4 << 20
F32 = jnp.float32
ROUNDS = 3


def with_halo(shard, sides, width):
    for axis, dim in sides:
        devices, length = (lax.axis_size(axis), shard.shape[dim])
        up = [(i, (i + 1) % devices) for i in range(devices - 1)]
        down = [(j, i) for i, j in up]
        last = lax.slice_in_dim(shard, length - width, length, axis=dim)
        first = lax.slice_in_dim(shard, 0, width, axis=dim)
        before = lax.ppermute(last, axis, up)
        after = lax.ppermute(first, axis, down)
        shard = jnp.concatenate([before, shard, after], axis=dim)
    return shard


def tap_sum(weights, padded, planes, height, breadth, equation, flipped):
    total = None
    for i in range(3):
        for j in range(3):
            for k in range(3):
                a, b, c = (2 - i, 2 - j, 2 - k) if flipped else (i, j, k)
                window = padded[:, a : a + planes, b : b + height, c : c + breadth]
                term = jnp.einsum(equation, weights[i, j, k], window, preferred_element_type=F32)
                total = term if total is None else total + term
    return total.astype(jnp.bfloat16)


def general_body(activations, cotangent, relu_mask, weights):
    planes, breadth = activations.shape[1], activations.shape[3]
    masked = jnp.where(relu_mask == 1, cotangent, jnp.zeros_like(cotangent))
    stacked = jnp.stack([activations, masked])
    patches = lax.all_to_all(stacked, "chan", split_axis=3, concat_axis=1, tiled=True)
    rimmed = with_halo(patches, (("chan", 3), ("slab", 2)), 1)
    padded = jnp.pad(rimmed, ((0, 0), (0, 0), (0, 0), (0, 0), (1, 1)))
    height = patches.shape[3]
    pre = tap_sum(weights, padded[0], planes, height, breadth, "oi,idhw->odhw", False)
    grad = tap_sum(weights, padded[1], planes, height, breadth, "oi,odhw->idhw", True)
    return tuple(
        lax.all_to_all(block, "chan", split_axis=0, concat_axis=2, tiled=True) for block in (pre, grad)
    )


def window(blocks, a, r, planes):
    sides = []
    for p in planes:
        pieces = []
        for row in (r - 1, r, r + 1):
            inside = 0 <= row < blocks[0].shape[1]
            pieces += [b[a, row, p] if inside else jnp.zeros(b.shape[3:], b.dtype) for b in blocks]
        sides.append(jnp.concatenate(pieces, axis=0))
    return sides[0] if len(sides) == 1 else jnp.concatenate(sides, axis=1)


def columns(taps):
    left, mid, right = taps
    lane = lax.broadcasted_iota(jnp.int32, mid.shape, 1)
    left = jnp.where(lane == 0, 0.0, pltpu.roll(left, 1, 1))
    right = jnp.where(lane == mid.shape[1] - 1, 0.0, pltpu.roll(right, mid.shape[1] - 1, 1))
    return left + mid + right


def all_planes(lhs, blocks, a, r, wanted):
    _, _, planes, width, cols = blocks[0].shape
    y = jnp.dot(lhs, window(blocks, a, r, range(planes)), preferred_element_type=F32)

    def part(t, k, p):
        top = (t * 3 + k) * width
        return y[top : top + width, p * cols : (p + 1) * cols]

    def plane(q):
        inputs = [p for p in range(planes) if 0 <= p - q + 1 <= 2]
        return columns([functools.reduce(jnp.add, [part(p - q + 1, k, p) for p in inputs]) for k in range(3)])

    return [plane(q) for q in wanted]


def early_kernel(count, lhs_ref, *refs):
    blocks, sum_ref = refs[:count], refs[count]
    arrays, rows, planes, width, _ = blocks[0].shape
    depth = 3 * count * width
    for a in range(arrays):
        lhs = lhs_ref[a, :, :depth]
        for r in range(rows):
            for q, value in enumerate(all_planes(lhs, blocks, a, r, range(-1, planes + 1))):
                sum_ref[a, r, q] = value


def edge_kernel(count, start, lhs_ref, sum_ref, *refs):
    blocks, edge_refs = refs[:count], refs[count:]
    arrays, rows, planes, width, _ = blocks[0].shape
    depth = 3 * count * width
    slab = lax.axis_index("slab")

    def edge(a, r, t, p):
        lhs = lhs_ref[a, t * 3 * width : (t + 1) * 3 * width, start : start + depth]
        y = jnp.dot(lhs, window(blocks, a, r, [p]), preferred_element_type=F32)
        return columns([y[k * width : (k + 1) * width] for k in range(3)])

    for a in range(arrays):
        for r in range(rows):
            below = edge(a, r, 2, 0) + sum_ref[a, r, 0]
            above = edge(a, r, 0, planes - 1) + sum_ref[a, r, planes + 1]
            for j, edge_ref in enumerate(edge_refs):
                edge_ref[a, r] = jnp.where(lax.rem(slab, ROUNDS) == j, above, below)


def inner_kernel(count, start, lhs_ref, sum_ref, *refs):
    blocks, inner_ref = refs[:count], refs[count]
    arrays, rows, planes, width, _ = blocks[0].shape
    depth = 3 * count * width
    for a in range(arrays):
        lhs = lhs_ref[a, :, start : start + depth]
        for r in range(rows):
            for p, value in enumerate(all_planes(lhs, blocks, a, r, range(planes))):
                inner_ref[a, r, p] = value + sum_ref[a, r, p + 1]


def add_kernel(inner_ref, *refs):
    edge_refs, (pre_ref, grad_ref, turned_ref) = refs[:ROUNDS], refs[ROUNDS:]
    _, rows, planes, width, cols = inner_ref.shape
    slab = lax.axis_index("slab")
    below, above = slab > 0, slab < lax.axis_size("slab") - 1

    def received(a, r, pair, exists):
        value = edge_refs[0][a, r]
        for j in range(1, ROUNDS):
            value = jnp.where(lax.rem(pair, ROUNDS) == j, edge_refs[j][a, r], value)
        return jnp.where(exists, value, 0.0)

    for a, out_ref in enumerate((pre_ref, grad_ref)):
        for p in range(planes):
            for r in range(rows):
                value = inner_ref[a, r, p]
                if p == 0:
                    value = value + received(a, r, slab + ROUNDS - 1, below)
                if p == planes - 1:
                    value = value + received(a, r, slab, above)
                turned_ref[pl.ds(r, width, stride=rows), :] = value
            out_ref[:, p] = turned_ref[...].reshape(width, rows, cols).astype(jnp.bfloat16)


def aligned_body(activations, cotangent, relu_mask, weights):
    width, planes, rows, cols = activations.shape
    devices, slabs = lax.axis_size("chan"), lax.axis_size("slab")
    channels = width * devices
    masked = jnp.where(relu_mask == 1, cotangent, jnp.zeros_like(cotangent))
    own = jnp.stack([activations, masked]).transpose(0, 3, 2, 1, 4)

    def swap(value, bit):
        return lax.ppermute(value, "chan", [(i, i ^ bit) for i in range(devices)])

    far = list(range(2, devices, 2))
    last = far.pop()
    early = [0, last]
    near = {bit: own if bit == 0 else swap(own, bit) for bit in early + far}

    me = lax.axis_index("chan")
    forward = lax.dynamic_slice_in_dim(weights, me * width, width, 3)
    backward = lax.dynamic_slice_in_dim(weights, me * width, width, 4)[::-1, ::-1, ::-1].swapaxes(3, 4)
    lhs = jnp.stack([forward, backward]).transpose(0, 1, 3, 4, 2, 5)
    lhs = lhs.reshape(2 * 9 * width, 3 * channels)
    column, start = [], 0
    for bits in (early, far):
        start = len(column)
        column += [
            (k, bit, i) for k in range(3) for near_bit in bits for bit in (near_bit, near_bit + 1) for i in range(width)
        ]
        column += [(3, 0, 0)] * (-len(column) % LANES)
    tap, bit, inside = (jnp.array(v, jnp.int32) for v in zip(*column))
    target = tap * channels + jnp.bitwise_xor(bit, me) * width + inside
    target = jnp.where(tap == 3, -1, target)
    order = (lax.broadcasted_iota(jnp.int32, (3 * channels, len(column)), 0) == target[None]).astype(jnp.bfloat16)
    lhs = jnp.dot(lhs, order, preferred_element_type=F32).astype(jnp.bfloat16).reshape(2, 9 * width, len(column))

    near[last], lhs = lax.optimization_barrier((near[last], lhs))
    blocks = {}
    for bit in early + far:
        blocks[bit] = near[bit]
        blocks[bit + 1] = swap(near[bit], 1)
    first = [blocks[bit + i] for bit in early for i in (0, 1)]
    second = [blocks[bit + i] for bit in far for i in (0, 1)]

    def call(kernel, out_shape, *args):
        return pl.pallas_call(
            kernel,
            out_shape=out_shape,
            in_specs=[pl.BlockSpec(memory_space=pltpu.VMEM)] * len(args),
            out_specs=jax.tree.map(lambda _: pl.BlockSpec(memory_space=pltpu.VMEM), out_shape),
            compiler_params=pltpu.CompilerParams(vmem_limit_bytes=CONV_VMEM),
            cost_estimate=pl.CostEstimate(flops=1 << 28, bytes_accessed=1 << 20, transcendentals=0),
        )(*args)

    def sums(*middle):
        return jax.ShapeDtypeStruct((2, rows, *middle, width, cols), F32)

    total = call(functools.partial(early_kernel, len(first)), sums(planes + 2), lhs, *first)
    edges = call(functools.partial(edge_kernel, len(second), start), (sums(),) * ROUNDS, lhs, total, *second)

    largest = 9 * channels * INPUT_MAX * WEIGHT_MAX
    scale = 2.0 ** math.floor(math.log2(float(jnp.finfo(jnp.float16).max) / largest))

    def exchange(value, turn):
        partner = {}
        for i in range(turn, slabs - 1, ROUNDS):
            partner[i], partner[i + 1] = i + 1, i
        pairs = [
            (c * slabs + s, c * slabs + partner[s] if s in partner else (c ^ 1) * slabs + s)
            for c in range(devices)
            for s in range(slabs)
        ]
        value = (value * scale).astype(jnp.float16)
        value = lax.ppermute(value, ("chan", "slab"), pairs)
        return value.astype(F32) * (1 / scale)

    edges = [exchange(value, turn) for turn, value in enumerate(edges)]
    inner = call(functools.partial(inner_kernel, len(second), start), sums(planes), lhs, total, *second)
    out = jax.ShapeDtypeStruct(activations.shape, jnp.bfloat16)
    return tuple(
        pl.pallas_call(
            add_kernel,
            out_shape=(out, out),
            in_specs=[pl.BlockSpec(memory_space=pltpu.VMEM)] * (ROUNDS + 1),
            out_specs=[pl.BlockSpec(memory_space=pltpu.VMEM)] * 2,
            scratch_shapes=[pltpu.VMEM((width * rows, cols), F32)],
            compiler_params=pltpu.CompilerParams(vmem_limit_bytes=ADD_VMEM),
            name="add",
        )(inner, *edges)
    )


def body(activations, cotangent, relu_mask, weights):
    width, planes, rows, cols = activations.shape
    devices = lax.axis_size("chan")
    aligned = (
        width % TILE == 0
        and cols == LANES
        and devices & (devices - 1) == 0
        and devices > 4
        and planes >= 2
        and rows % 8 == 0
        and lax.axis_size("slab") > 1
    )
    if not aligned:
        return general_body(activations, cotangent, relu_mask, weights)
    return aligned_body(activations, cotangent, relu_mask, weights)


def solution(mesh):
    placed = P("chan", "slab", None, None)
    return jax.shard_map(
        body,
        mesh=mesh,
        in_specs=(placed, placed, placed, P()),
        out_specs=(placed, placed),
        check_vma=False,
    )
```

```python
import functools
import math

import jax
import jax.numpy as jnp
from jax import lax
from jax.experimental import pallas as pl
from jax.experimental.pallas import tpu as pltpu
from jax.sharding import PartitionSpec as P


LANES = 128
TILE = 16
INPUT_MAX, WEIGHT_MAX = 6.0, 0.109375
CONV_VMEM, ADD_VMEM = 8 << 20, 4 << 20
F32 = jnp.float32
ROUNDS = 3


def with_halo(shard, sides, width):
    for axis, dim in sides:
        devices, length = (lax.axis_size(axis), shard.shape[dim])
        up = [(i, (i + 1) % devices) for i in range(devices - 1)]
        down = [(j, i) for i, j in up]
        last = lax.slice_in_dim(shard, length - width, length, axis=dim)
        first = lax.slice_in_dim(shard, 0, width, axis=dim)
        before = lax.ppermute(last, axis, up)
        after = lax.ppermute(first, axis, down)
        shard = jnp.concatenate([before, shard, after], axis=dim)
    return shard


def tap_sum(weights, padded, planes, height, breadth, equation, flipped):
    total = None
    for i in range(3):
        for j in range(3):
            for k in range(3):
                a, b, c = (2 - i, 2 - j, 2 - k) if flipped else (i, j, k)
                window = padded[:, a : a + planes, b : b + height, c : c + breadth]
                term = jnp.einsum(equation, weights[i, j, k], window, preferred_element_type=F32)
                total = term if total is None else total + term
    return total.astype(jnp.bfloat16)


def general_body(activations, cotangent, relu_mask, weights):
    planes, breadth = activations.shape[1], activations.shape[3]
    masked = jnp.where(relu_mask == 1, cotangent, jnp.zeros_like(cotangent))
    stacked = jnp.stack([activations, masked])
    patches = lax.all_to_all(stacked, "chan", split_axis=3, concat_axis=1, tiled=True)
    rimmed = with_halo(patches, (("chan", 3), ("slab", 2)), 1)
    padded = jnp.pad(rimmed, ((0, 0), (0, 0), (0, 0), (0, 0), (1, 1)))
    height = patches.shape[3]
    pre = tap_sum(weights, padded[0], planes, height, breadth, "oi,idhw->odhw", False)
    grad = tap_sum(weights, padded[1], planes, height, breadth, "oi,odhw->idhw", True)
    return tuple(
        lax.all_to_all(block, "chan", split_axis=0, concat_axis=2, tiled=True) for block in (pre, grad)
    )


def window(blocks, a, r, planes):
    sides = []
    for p in planes:
        pieces = []
        for row in (r - 1, r, r + 1):
            inside = 0 <= row < blocks[0].shape[1]
            pieces += [b[a, row, p] if inside else jnp.zeros(b.shape[3:], b.dtype) for b in blocks]
        sides.append(jnp.concatenate(pieces, axis=0))
    return sides[0] if len(sides) == 1 else jnp.concatenate(sides, axis=1)


def columns(taps):
    left, mid, right = taps
    lane = lax.broadcasted_iota(jnp.int32, mid.shape, 1)
    left = jnp.where(lane == 0, 0.0, pltpu.roll(left, 1, 1))
    right = jnp.where(lane == mid.shape[1] - 1, 0.0, pltpu.roll(right, mid.shape[1] - 1, 1))
    return left + mid + right


def all_planes(lhs, blocks, a, r, wanted):
    _, _, planes, width, cols = blocks[0].shape
    y = jnp.dot(lhs, window(blocks, a, r, range(planes)), preferred_element_type=F32)

    def part(t, k, p):
        top = (t * 3 + k) * width
        return y[top : top + width, p * cols : (p + 1) * cols]

    def plane(q):
        inputs = [p for p in range(planes) if 0 <= p - q + 1 <= 2]
        return columns([functools.reduce(jnp.add, [part(p - q + 1, k, p) for p in inputs]) for k in range(3)])

    return [plane(q) for q in wanted]


def early_kernel(count, lhs_ref, *refs):
    blocks, sum_ref = refs[:count], refs[count]
    arrays, rows, planes, width, _ = blocks[0].shape
    depth = 3 * count * width
    for a in range(arrays):
        lhs = lhs_ref[a, :, :depth]
        for r in range(rows):
            for q, value in enumerate(all_planes(lhs, blocks, a, r, range(-1, planes + 1))):
                sum_ref[a, r, q] = value


def edge_kernel(count, start, lhs_ref, sum_ref, *refs):
    blocks, edge_refs = refs[:count], refs[count:]
    arrays, rows, planes, width, cols = blocks[0].shape
    depth = 3 * count * width
    slab = lax.axis_index("slab")

    for a in range(arrays):
        taps = [lhs_ref[a, t * 3 * width : (t + 1) * 3 * width, start : start + depth] for t in (2, 0)]
        lhs = jnp.concatenate(taps, axis=0)
        for r in range(rows):
            y = jnp.dot(lhs, window(blocks, a, r, (0, planes - 1)), preferred_element_type=F32)
            below, above = (
                columns([y[(3 * i + k) * width : (3 * i + k + 1) * width, i * cols : (i + 1) * cols] for k in range(3)])
                for i in range(2)
            )
            below = below + sum_ref[a, r, 0]
            above = above + sum_ref[a, r, planes + 1]
            for j, edge_ref in enumerate(edge_refs):
                edge_ref[a, r] = jnp.where(lax.rem(slab, ROUNDS) == j, above, below)


def inner_kernel(count, start, lhs_ref, sum_ref, *refs):
    blocks, inner_ref = refs[:count], refs[count]
    arrays, rows, planes, width, _ = blocks[0].shape
    depth = 3 * count * width
    for a in range(arrays):
        lhs = lhs_ref[a, :, start : start + depth]
        for r in range(rows):
            for p, value in enumerate(all_planes(lhs, blocks, a, r, range(planes))):
                inner_ref[a, r, p] = value + sum_ref[a, r, p + 1]


def add_kernel(inner_ref, *refs):
    edge_refs, (pre_ref, grad_ref, turned_ref) = refs[:ROUNDS], refs[ROUNDS:]
    _, rows, planes, width, cols = inner_ref.shape
    slab = lax.axis_index("slab")
    below, above = slab > 0, slab < lax.axis_size("slab") - 1

    def received(a, r, pair, exists):
        value = edge_refs[0][a, r]
        for j in range(1, ROUNDS):
            value = jnp.where(lax.rem(pair, ROUNDS) == j, edge_refs[j][a, r], value)
        return jnp.where(exists, value, 0.0)

    for a, out_ref in enumerate((pre_ref, grad_ref)):
        for p in range(planes):
            for r in range(rows):
                value = inner_ref[a, r, p]
                if p == 0:
                    value = value + received(a, r, slab + ROUNDS - 1, below)
                if p == planes - 1:
                    value = value + received(a, r, slab, above)
                turned_ref[pl.ds(r, width, stride=rows), :] = value
            out_ref[:, p] = turned_ref[...].reshape(width, rows, cols).astype(jnp.bfloat16)


def aligned_body(activations, cotangent, relu_mask, weights):
    width, planes, rows, cols = activations.shape
    devices, slabs = lax.axis_size("chan"), lax.axis_size("slab")
    channels = width * devices
    masked = jnp.where(relu_mask == 1, cotangent, jnp.zeros_like(cotangent))
    own = jnp.stack([activations, masked]).transpose(0, 3, 2, 1, 4)

    def swap(value, bit):
        return lax.ppermute(value, "chan", [(i, i ^ bit) for i in range(devices)])

    far = list(range(2, devices, 2))
    last = far.pop()
    early = [0, last]
    near = {bit: own if bit == 0 else swap(own, bit) for bit in early + far}

    me = lax.axis_index("chan")
    forward = lax.dynamic_slice_in_dim(weights, me * width, width, 3)
    backward = lax.dynamic_slice_in_dim(weights, me * width, width, 4)[::-1, ::-1, ::-1].swapaxes(3, 4)
    lhs = jnp.stack([forward, backward]).transpose(0, 1, 3, 4, 2, 5)
    lhs = lhs.reshape(2 * 9 * width, 3 * channels)
    column, start = [], 0
    for bits in (early, far):
        start = len(column)
        column += [
            (k, bit, i) for k in range(3) for near_bit in bits for bit in (near_bit, near_bit + 1) for i in range(width)
        ]
        column += [(3, 0, 0)] * (-len(column) % LANES)
    tap, bit, inside = (jnp.array(v, jnp.int32) for v in zip(*column))
    target = tap * channels + jnp.bitwise_xor(bit, me) * width + inside
    target = jnp.where(tap == 3, -1, target)
    order = (lax.broadcasted_iota(jnp.int32, (3 * channels, len(column)), 0) == target[None]).astype(jnp.bfloat16)
    lhs = jnp.dot(lhs, order, preferred_element_type=F32).astype(jnp.bfloat16).reshape(2, 9 * width, len(column))

    near[last], lhs = lax.optimization_barrier((near[last], lhs))
    blocks = {}
    for bit in early + far:
        blocks[bit] = near[bit]
        blocks[bit + 1] = swap(near[bit], 1)
    first = [blocks[bit + i] for bit in early for i in (0, 1)]
    second = [blocks[bit + i] for bit in far for i in (0, 1)]

    def call(kernel, out_shape, *args):
        return pl.pallas_call(
            kernel,
            out_shape=out_shape,
            in_specs=[pl.BlockSpec(memory_space=pltpu.VMEM)] * len(args),
            out_specs=jax.tree.map(lambda _: pl.BlockSpec(memory_space=pltpu.VMEM), out_shape),
            compiler_params=pltpu.CompilerParams(vmem_limit_bytes=CONV_VMEM),
            cost_estimate=pl.CostEstimate(flops=1 << 28, bytes_accessed=1 << 20, transcendentals=0),
        )(*args)

    def sums(*middle):
        return jax.ShapeDtypeStruct((2, rows, *middle, width, cols), F32)

    total = call(functools.partial(early_kernel, len(first)), sums(planes + 2), lhs, *first)
    edges = call(functools.partial(edge_kernel, len(second), start), (sums(),) * ROUNDS, lhs, total, *second)

    largest = 9 * channels * INPUT_MAX * WEIGHT_MAX
    scale = 2.0 ** math.floor(math.log2(float(jnp.finfo(jnp.float16).max) / largest))

    def exchange(value, turn):
        partner = {}
        for i in range(turn, slabs - 1, ROUNDS):
            partner[i], partner[i + 1] = i + 1, i
        pairs = [
            (c * slabs + s, c * slabs + partner[s] if s in partner else (c ^ 1) * slabs + s)
            for c in range(devices)
            for s in range(slabs)
        ]
        value = (value * scale).astype(jnp.float16)
        value = lax.ppermute(value, ("chan", "slab"), pairs)
        return value.astype(F32) * (1 / scale)

    edges = [exchange(value, turn) for turn, value in enumerate(edges)]
    inner = call(functools.partial(inner_kernel, len(second), start), sums(planes), lhs, total, *second)
    out = jax.ShapeDtypeStruct(activations.shape, jnp.bfloat16)
    return tuple(
        pl.pallas_call(
            add_kernel,
            out_shape=(out, out),
            in_specs=[pl.BlockSpec(memory_space=pltpu.VMEM)] * (ROUNDS + 1),
            out_specs=[pl.BlockSpec(memory_space=pltpu.VMEM)] * 2,
            scratch_shapes=[pltpu.VMEM((width * rows, cols), F32)],
            compiler_params=pltpu.CompilerParams(vmem_limit_bytes=ADD_VMEM),
            name="add",
        )(inner, *edges)
    )


def body(activations, cotangent, relu_mask, weights):
    width, planes, rows, cols = activations.shape
    devices = lax.axis_size("chan")
    aligned = (
        width % TILE == 0
        and cols == LANES
        and devices & (devices - 1) == 0
        and devices > 4
        and planes >= 2
        and rows % 8 == 0
        and lax.axis_size("slab") > 1
    )
    if not aligned:
        return general_body(activations, cotangent, relu_mask, weights)
    return aligned_body(activations, cotangent, relu_mask, weights)


def solution(mesh):
    placed = P("chan", "slab", None, None)
    return jax.shard_map(
        body,
        mesh=mesh,
        in_specs=(placed, placed, placed, P()),
        out_specs=(placed, placed),
        check_vma=False,
    )
```

```python
import functools
import math

import jax
import jax.numpy as jnp
from jax import lax
from jax.experimental import pallas as pl
from jax.experimental.pallas import tpu as pltpu
from jax.sharding import PartitionSpec as P


LANES = 128
TILE = 16
INPUT_MAX, WEIGHT_MAX = 6.0, 0.109375
CONV_VMEM, ADD_VMEM = 8 << 20, 4 << 20
F32 = jnp.float32
PIECES = 2
ROUNDS = 3


def with_halo(shard, sides, width):
    for axis, dim in sides:
        devices, length = (lax.axis_size(axis), shard.shape[dim])
        up = [(i, (i + 1) % devices) for i in range(devices - 1)]
        down = [(j, i) for i, j in up]
        last = lax.slice_in_dim(shard, length - width, length, axis=dim)
        first = lax.slice_in_dim(shard, 0, width, axis=dim)
        before = lax.ppermute(last, axis, up)
        after = lax.ppermute(first, axis, down)
        shard = jnp.concatenate([before, shard, after], axis=dim)
    return shard


def tap_sum(weights, padded, planes, height, breadth, equation, flipped):
    total = None
    for i in range(3):
        for j in range(3):
            for k in range(3):
                a, b, c = (2 - i, 2 - j, 2 - k) if flipped else (i, j, k)
                window = padded[:, a : a + planes, b : b + height, c : c + breadth]
                term = jnp.einsum(equation, weights[i, j, k], window, preferred_element_type=F32)
                total = term if total is None else total + term
    return total.astype(jnp.bfloat16)


def general_body(activations, cotangent, relu_mask, weights):
    planes, breadth = activations.shape[1], activations.shape[3]
    masked = jnp.where(relu_mask == 1, cotangent, jnp.zeros_like(cotangent))
    stacked = jnp.stack([activations, masked])
    patches = lax.all_to_all(stacked, "chan", split_axis=3, concat_axis=1, tiled=True)
    rimmed = with_halo(patches, (("chan", 3), ("slab", 2)), 1)
    padded = jnp.pad(rimmed, ((0, 0), (0, 0), (0, 0), (0, 0), (1, 1)))
    height = patches.shape[3]
    pre = tap_sum(weights, padded[0], planes, height, breadth, "oi,idhw->odhw", False)
    grad = tap_sum(weights, padded[1], planes, height, breadth, "oi,odhw->idhw", True)
    return tuple(
        lax.all_to_all(block, "chan", split_axis=0, concat_axis=2, tiled=True) for block in (pre, grad)
    )


def window(blocks, a, places):
    sides = []
    for r, p in places:
        pieces = []
        for row in (r - 1, r, r + 1):
            inside = 0 <= row < blocks[0].shape[1]
            pieces += [b[a, row, p] if inside else jnp.zeros(b.shape[3:], b.dtype) for b in blocks]
        sides.append(jnp.concatenate(pieces, axis=0))
    return jnp.concatenate(sides, axis=1)


def columns(taps):
    left, mid, right = taps
    lane = lax.broadcasted_iota(jnp.int32, mid.shape, 1)
    left = jnp.where(lane == 0, 0.0, pltpu.roll(left, 1, 1))
    right = jnp.where(lane == mid.shape[1] - 1, 0.0, pltpu.roll(right, mid.shape[1] - 1, 1))
    return left + mid + right


def all_planes(lhs, blocks, a, r, wanted):
    _, _, planes, width, cols = blocks[0].shape
    y = jnp.dot(lhs, window(blocks, a, [(r, p) for p in range(planes)]), preferred_element_type=F32)

    def part(t, k, p):
        top = (t * 3 + k) * width
        return y[top : top + width, p * cols : (p + 1) * cols]

    def plane(q):
        inputs = [p for p in range(planes) if 0 <= p - q + 1 <= 2]
        return columns([functools.reduce(jnp.add, [part(p - q + 1, k, p) for p in inputs]) for k in range(3)])

    return [plane(q) for q in wanted]


def pack_kernel(act_hbm, cot_hbm, mask_hbm, own_ref, act_ref, cot_ref, mask_ref, turned_ref, sems):
    width, planes, rows, cols = act_ref.shape
    pairs = ((act_hbm, act_ref), (cot_hbm, cot_ref), (mask_hbm, mask_ref))
    step = width // PIECES
    copies = [
        [
            pltpu.make_async_copy(source.at[pl.ds(k * step, step)], target.at[pl.ds(k * step, step)], sems.at[i, k])
            for k in range(PIECES)
        ]
        for i, (source, target) in enumerate(pairs)
    ]
    for i in (2, 0, 1):
        for k in range(PIECES):
            copies[i][k].start()

    def turn(a):
        for p in range(planes):
            value = (act_ref, cot_ref)[a][:, p].astype(F32)
            if a == 1:
                value = jnp.where(mask_ref[:, p] == 1, value, 0.0)
            turned_ref[a, p] = value.reshape(width * rows, cols)
            for r in range(rows):
                own_ref[a, r, p] = turned_ref[a, p, pl.ds(r, width, stride=rows), :].astype(jnp.bfloat16)

    for copy in copies[0]:
        copy.wait()
    turn(0)
    for copy in copies[1] + copies[2]:
        copy.wait()
    turn(1)


def load_kernel(weights_hbm, own_ref, weights_ref, sem):
    copy = pltpu.make_async_copy(weights_hbm, weights_ref, sem)
    copy.start()
    copy.wait()


def early_kernel(count, lhs_ref, *refs):
    blocks, sum_ref = refs[:count], refs[count]
    arrays, rows, planes, width, _ = blocks[0].shape
    depth = 3 * count * width
    for a in range(arrays):
        lhs = lhs_ref[a, :, :depth]
        for r in range(rows):
            for q, value in enumerate(all_planes(lhs, blocks, a, r, range(-1, planes + 1))):
                sum_ref[a, r, q] = value


def edge_kernel(count, start, first, lhs_ref, sum_ref, *refs):
    blocks, edge_ref = refs[:count], refs[count]
    arrays, rows, planes, width, cols = blocks[0].shape
    depth, height = 3 * count * width, 3 * width
    above = (lax.rem(lax.axis_index("slab"), ROUNDS) == 0) == first
    p, q = jnp.where(above, planes - 1, 0), jnp.where(above, planes + 1, 0)
    top = pl.multiple_of(jnp.where(above, 0, 2 * height), TILE)
    for a in range(arrays):
        lhs = lhs_ref[a, pl.ds(top, height), start : start + depth]
        for r in range(0, rows, 2):
            y = jnp.dot(lhs, window(blocks, a, [(r, p), (r + 1, p)]), preferred_element_type=F32)
            for i in range(2):
                taps = [y[k * width : (k + 1) * width, i * cols : (i + 1) * cols] for k in range(3)]
                edge_ref[a, r + i] = columns(taps) + sum_ref[a, r + i, q]


def inner_kernel(count, start, lhs_ref, sum_ref, *refs):
    blocks, inner_ref = refs[:count], refs[count]
    arrays, rows, planes, width, _ = blocks[0].shape
    depth = 3 * count * width
    for a in range(arrays):
        lhs = lhs_ref[a, :, start : start + depth]
        for r in range(rows):
            for p, value in enumerate(all_planes(lhs, blocks, a, r, range(planes))):
                inner_ref[a, r, p] = value + sum_ref[a, r, p + 1]


def add_kernel(inner_ref, *refs):
    edge_refs, (pre_ref, grad_ref, turned_ref) = refs[:ROUNDS], refs[ROUNDS:]
    _, rows, planes, width, cols = inner_ref.shape
    slab = lax.axis_index("slab")
    below, above = slab > 0, slab < lax.axis_size("slab") - 1

    def received(a, r, pair, exists):
        value = edge_refs[0][a, r]
        for j in range(1, ROUNDS):
            value = jnp.where(lax.rem(pair, ROUNDS) == j, edge_refs[j][a, r], value)
        return jnp.where(exists, value, 0.0)

    for a, out_ref in enumerate((pre_ref, grad_ref)):
        for p in range(planes):
            for r in range(rows):
                value = inner_ref[a, r, p]
                if p == 0:
                    value = value + received(a, r, slab + ROUNDS - 1, below)
                if p == planes - 1:
                    value = value + received(a, r, slab, above)
                turned_ref[pl.ds(r, width, stride=rows), :] = value
            out_ref[:, p] = turned_ref[...].reshape(width, rows, cols).astype(jnp.bfloat16)


def aligned_body(activations, cotangent, relu_mask, weights):
    width, planes, rows, cols = activations.shape
    devices, slabs = lax.axis_size("chan"), lax.axis_size("slab")
    channels = width * devices
    own = pl.pallas_call(
        pack_kernel,
        out_shape=jax.ShapeDtypeStruct((2, rows, planes, width, cols), jnp.bfloat16),
        in_specs=[pl.BlockSpec(memory_space=pltpu.HBM)] * 3,
        out_specs=pl.BlockSpec(memory_space=pltpu.VMEM),
        scratch_shapes=[pltpu.VMEM(v.shape, v.dtype) for v in (activations, cotangent, relu_mask)]
        + [pltpu.VMEM((2, planes, width * rows, cols), F32), pltpu.SemaphoreType.DMA((3, PIECES))],
        compiler_params=pltpu.CompilerParams(vmem_limit_bytes=ADD_VMEM),
        name="pack",
    )(*(pltpu.with_memory_space_constraint(v, pltpu.HBM) for v in (activations, cotangent, relu_mask)))

    def swap(value, bit):
        return lax.ppermute(value, "chan", [(i, i ^ bit) for i in range(devices)])

    far = list(range(2, devices, 2))
    last = far.pop()
    early = [0, last]
    far.reverse()
    near = {bit: own if bit == 0 else swap(own, bit) for bit in early + far}

    weights = pl.pallas_call(
        load_kernel,
        out_shape=jax.ShapeDtypeStruct(weights.shape, weights.dtype),
        in_specs=[pl.BlockSpec(memory_space=pltpu.HBM), pl.BlockSpec(memory_space=pl.ANY)],
        out_specs=pl.BlockSpec(memory_space=pltpu.VMEM),
        scratch_shapes=[pltpu.SemaphoreType.DMA],
        compiler_params=pltpu.CompilerParams(vmem_limit_bytes=ADD_VMEM),
        name="load",
    )(pltpu.with_memory_space_constraint(weights, pltpu.HBM), own)

    me = lax.axis_index("chan")
    forward = lax.dynamic_slice_in_dim(weights, me * width, width, 3)
    backward = lax.dynamic_slice_in_dim(weights, me * width, width, 4)[::-1, ::-1, ::-1].swapaxes(3, 4)
    lhs = jnp.stack([forward, backward]).transpose(0, 1, 3, 4, 2, 5)
    lhs = lhs.reshape(2 * 9 * width, 3 * channels)
    column, start = [], 0
    for bits in (early, far):
        start = len(column)
        column += [
            (k, bit, i) for k in range(3) for near_bit in bits for bit in (near_bit, near_bit + 1) for i in range(width)
        ]
        column += [(3, 0, 0)] * (-len(column) % LANES)
    tap, bit, inside = (jnp.array(v, jnp.int32) for v in zip(*column))
    target = tap * channels + jnp.bitwise_xor(bit, me) * width + inside
    target = jnp.where(tap == 3, -1, target)
    order = (lax.broadcasted_iota(jnp.int32, (3 * channels, len(column)), 0) == target[None]).astype(jnp.bfloat16)
    lhs = jnp.dot(lhs, order, preferred_element_type=F32).astype(jnp.bfloat16).reshape(2, 9 * width, len(column))

    near[last], lhs = lax.optimization_barrier((near[last], lhs))
    blocks = {}
    for bit in early + far:
        blocks[bit] = near[bit]
        blocks[bit + 1] = swap(near[bit], 1)
    first = [blocks[bit + i] for bit in early for i in (0, 1)]
    second = [blocks[bit + i] for bit in far for i in (0, 1)]

    def call(kernel, out_shape, *args):
        return pl.pallas_call(
            kernel,
            out_shape=out_shape,
            in_specs=[pl.BlockSpec(memory_space=pltpu.VMEM)] * len(args),
            out_specs=jax.tree.map(lambda _: pl.BlockSpec(memory_space=pltpu.VMEM), out_shape),
            compiler_params=pltpu.CompilerParams(vmem_limit_bytes=CONV_VMEM),
            cost_estimate=pl.CostEstimate(flops=1 << 28, bytes_accessed=1 << 20, transcendentals=0),
        )(*args)

    def sums(*middle):
        return jax.ShapeDtypeStruct((2, rows, *middle, width, cols), F32)

    total = call(functools.partial(early_kernel, len(first)), sums(planes + 2), lhs, *first)
    largest = 9 * channels * INPUT_MAX * WEIGHT_MAX
    scale = 2.0 ** math.floor(math.log2(float(jnp.finfo(jnp.float16).max) / largest))

    def exchange(value, turn):
        partner = {}
        for i in range(turn, slabs - 1, ROUNDS):
            partner[i], partner[i + 1] = i + 1, i
        pairs = [
            (c * slabs + s, c * slabs + partner[s] if s in partner else (c ^ 1) * slabs + s)
            for c in range(devices)
            for s in range(slabs)
        ]
        value = (value * scale).astype(jnp.float16)
        value = lax.ppermute(value, ("chan", "slab"), pairs)
        return value.astype(F32) * (1 / scale)

    sent, other = (
        call(functools.partial(edge_kernel, len(second), start, i == 0), sums(), lhs, total, *second)
        for i in range(2)
    )
    again, other = lax.optimization_barrier((sent, other))
    between = jnp.where(lax.rem(lax.axis_index("slab"), ROUNDS) == 2, again, other)
    edges = [exchange(value, turn) for turn, value in enumerate((sent, between, other))]
    inner = call(functools.partial(inner_kernel, len(second), start), sums(planes), lhs, total, *second)
    out = jax.ShapeDtypeStruct(activations.shape, jnp.bfloat16)
    return tuple(
        pl.pallas_call(
            add_kernel,
            out_shape=(out, out),
            in_specs=[pl.BlockSpec(memory_space=pltpu.VMEM)] * (ROUNDS + 1),
            out_specs=[pl.BlockSpec(memory_space=pltpu.VMEM)] * 2,
            scratch_shapes=[pltpu.VMEM((width * rows, cols), F32)],
            compiler_params=pltpu.CompilerParams(vmem_limit_bytes=ADD_VMEM),
            name="add",
        )(inner, *edges)
    )


def body(activations, cotangent, relu_mask, weights):
    width, planes, rows, cols = activations.shape
    devices = lax.axis_size("chan")
    aligned = (
        width % TILE == 0
        and cols == LANES
        and devices & (devices - 1) == 0
        and devices > 4
        and planes >= 2
        and rows % 8 == 0
        and lax.axis_size("slab") > 1
    )
    if not aligned:
        return general_body(activations, cotangent, relu_mask, weights)
    return aligned_body(activations, cotangent, relu_mask, weights)


def solution(mesh):
    placed = P("chan", "slab", None, None)
    return jax.shard_map(
        body,
        mesh=mesh,
        in_specs=(placed, placed, placed, P()),
        out_specs=(placed, placed),
        check_vma=False,
    )
```

```python
import functools
import math

import jax
import jax.numpy as jnp
from jax import lax
from jax.experimental import pallas as pl
from jax.experimental.pallas import tpu as pltpu
from jax.sharding import PartitionSpec as P


LANES = 128
TILE = 16
INPUT_MAX, WEIGHT_MAX = 6.0, 0.109375
CONV_VMEM, ADD_VMEM = 8 << 20, 4 << 20
F32 = jnp.float32
PIECES = 2
ROUNDS = 3


def with_halo(shard, sides, width):
    for axis, dim in sides:
        devices, length = (lax.axis_size(axis), shard.shape[dim])
        up = [(i, (i + 1) % devices) for i in range(devices - 1)]
        down = [(j, i) for i, j in up]
        last = lax.slice_in_dim(shard, length - width, length, axis=dim)
        first = lax.slice_in_dim(shard, 0, width, axis=dim)
        before = lax.ppermute(last, axis, up)
        after = lax.ppermute(first, axis, down)
        shard = jnp.concatenate([before, shard, after], axis=dim)
    return shard


def tap_sum(weights, padded, planes, height, breadth, equation, flipped):
    total = None
    for i in range(3):
        for j in range(3):
            for k in range(3):
                a, b, c = (2 - i, 2 - j, 2 - k) if flipped else (i, j, k)
                window = padded[:, a : a + planes, b : b + height, c : c + breadth]
                term = jnp.einsum(equation, weights[i, j, k], window, preferred_element_type=F32)
                total = term if total is None else total + term
    return total.astype(jnp.bfloat16)


def general_body(activations, cotangent, relu_mask, weights):
    planes, breadth = activations.shape[1], activations.shape[3]
    masked = jnp.where(relu_mask == 1, cotangent, jnp.zeros_like(cotangent))
    stacked = jnp.stack([activations, masked])
    patches = lax.all_to_all(stacked, "chan", split_axis=3, concat_axis=1, tiled=True)
    rimmed = with_halo(patches, (("chan", 3), ("slab", 2)), 1)
    padded = jnp.pad(rimmed, ((0, 0), (0, 0), (0, 0), (0, 0), (1, 1)))
    height = patches.shape[3]
    pre = tap_sum(weights, padded[0], planes, height, breadth, "oi,idhw->odhw", False)
    grad = tap_sum(weights, padded[1], planes, height, breadth, "oi,odhw->idhw", True)
    return tuple(
        lax.all_to_all(block, "chan", split_axis=0, concat_axis=2, tiled=True) for block in (pre, grad)
    )


def window(blocks, a, places):
    sides = []
    for r, p in places:
        pieces = []
        for row in (r - 1, r, r + 1):
            inside = 0 <= row < blocks[0].shape[1]
            pieces += [b[a, row, p] if inside else jnp.zeros(b.shape[3:], b.dtype) for b in blocks]
        sides.append(jnp.concatenate(pieces, axis=0))
    return jnp.concatenate(sides, axis=1)


def columns(taps):
    left, mid, right = taps
    lane = lax.broadcasted_iota(jnp.int32, mid.shape, 1)
    left = jnp.where(lane == 0, 0.0, pltpu.roll(left, 1, 1))
    right = jnp.where(lane == mid.shape[1] - 1, 0.0, pltpu.roll(right, mid.shape[1] - 1, 1))
    return left + mid + right


def all_planes(lhs, blocks, a, r, wanted):
    _, _, planes, width, cols = blocks[0].shape
    y = jnp.dot(lhs, window(blocks, a, [(r, p) for p in range(planes)]), preferred_element_type=F32)

    def part(t, k, p):
        top = (t * 3 + k) * width
        return y[top : top + width, p * cols : (p + 1) * cols]

    def plane(q):
        inputs = [p for p in range(planes) if 0 <= p - q + 1 <= 2]
        return columns([functools.reduce(jnp.add, [part(p - q + 1, k, p) for p in inputs]) for k in range(3)])

    return [plane(q) for q in wanted]


def pack_kernel(act_hbm, cot_hbm, mask_hbm, own_ref, act_ref, cot_ref, mask_ref, turned_ref, sems):
    width, planes, rows, cols = act_ref.shape
    pairs = ((act_hbm, act_ref), (cot_hbm, cot_ref), (mask_hbm, mask_ref))
    step = width // PIECES
    copies = [
        [
            pltpu.make_async_copy(source.at[pl.ds(k * step, step)], target.at[pl.ds(k * step, step)], sems.at[i, k])
            for k in range(PIECES)
        ]
        for i, (source, target) in enumerate(pairs)
    ]
    for i in (2, 0, 1):
        for k in range(PIECES):
            copies[i][k].start()

    def turn(a):
        for p in range(planes):
            value = (act_ref, cot_ref)[a][:, p].astype(F32)
            if a == 1:
                value = jnp.where(mask_ref[:, p] == 1, value, 0.0)
            turned_ref[a, p] = value.reshape(width * rows, cols)
            for r in range(rows):
                own_ref[a, r, p] = turned_ref[a, p, pl.ds(r, width, stride=rows), :].astype(jnp.bfloat16)

    for copy in copies[0]:
        copy.wait()
    turn(0)
    for copy in copies[1] + copies[2]:
        copy.wait()
    turn(1)


def load_kernel(weights_hbm, own_ref, weights_ref, sem):
    copy = pltpu.make_async_copy(weights_hbm, weights_ref, sem)
    copy.start()
    copy.wait()


def early_kernel(count, lhs_ref, *refs):
    blocks, sum_ref = refs[:count], refs[count]
    arrays, rows, planes, width, _ = blocks[0].shape
    depth = 3 * count * width
    for a in range(arrays):
        lhs = lhs_ref[a, :, :depth]
        for r in range(rows):
            for q, value in enumerate(all_planes(lhs, blocks, a, r, range(-1, planes + 1))):
                sum_ref[a, r, q] = value


def edge_kernel(count, start, lhs_ref, sum_ref, *refs):
    blocks, (first_ref, other_ref) = refs[:count], refs[count:]
    arrays, rows, planes, width, cols = blocks[0].shape
    depth = 3 * count * width
    upward = lax.rem(lax.axis_index("slab"), ROUNDS) == 0
    for a in range(arrays):
        taps = [lhs_ref[a, t * 3 * width : (t + 1) * 3 * width, start : start + depth] for t in (2, 0)]
        lhs = jnp.concatenate(taps, axis=0)
        for r in range(rows):
            y = jnp.dot(lhs, window(blocks, a, [(r, 0), (r, planes - 1)]), preferred_element_type=F32)
            below, above = (
                columns([y[(3 * i + k) * width : (3 * i + k + 1) * width, i * cols : (i + 1) * cols] for k in range(3)])
                for i in range(2)
            )
            below = below + sum_ref[a, r, 0]
            above = above + sum_ref[a, r, planes + 1]
            first_ref[a, r] = jnp.where(upward, above, below)
            other_ref[a, r] = jnp.where(upward, below, above)


def inner_kernel(count, start, lhs_ref, sum_ref, *refs):
    blocks, inner_ref = refs[:count], refs[count]
    arrays, rows, planes, width, _ = blocks[0].shape
    depth = 3 * count * width
    for a in range(arrays):
        lhs = lhs_ref[a, :, start : start + depth]
        for r in range(rows):
            for p, value in enumerate(all_planes(lhs, blocks, a, r, range(planes))):
                inner_ref[a, r, p] = value + sum_ref[a, r, p + 1]


def add_kernel(inner_ref, *refs):
    edge_refs, (pre_ref, grad_ref, turned_ref) = refs[:ROUNDS], refs[ROUNDS:]
    _, rows, planes, width, cols = inner_ref.shape
    slab = lax.axis_index("slab")
    below, above = slab > 0, slab < lax.axis_size("slab") - 1

    def received(a, r, pair, exists):
        value = edge_refs[0][a, r]
        for j in range(1, ROUNDS):
            value = jnp.where(lax.rem(pair, ROUNDS) == j, edge_refs[j][a, r], value)
        return jnp.where(exists, value, 0.0)

    for a, out_ref in enumerate((pre_ref, grad_ref)):
        for p in range(planes):
            for r in range(rows):
                value = inner_ref[a, r, p]
                if p == 0:
                    value = value + received(a, r, slab + ROUNDS - 1, below)
                if p == planes - 1:
                    value = value + received(a, r, slab, above)
                turned_ref[pl.ds(r, width, stride=rows), :] = value
            out_ref[:, p] = turned_ref[...].reshape(width, rows, cols).astype(jnp.bfloat16)


def aligned_body(activations, cotangent, relu_mask, weights):
    width, planes, rows, cols = activations.shape
    devices, slabs = lax.axis_size("chan"), lax.axis_size("slab")
    channels = width * devices
    own = pl.pallas_call(
        pack_kernel,
        out_shape=jax.ShapeDtypeStruct((2, rows, planes, width, cols), jnp.bfloat16),
        in_specs=[pl.BlockSpec(memory_space=pltpu.HBM)] * 3,
        out_specs=pl.BlockSpec(memory_space=pltpu.VMEM),
        scratch_shapes=[pltpu.VMEM(v.shape, v.dtype) for v in (activations, cotangent, relu_mask)]
        + [pltpu.VMEM((2, planes, width * rows, cols), F32), pltpu.SemaphoreType.DMA((3, PIECES))],
        compiler_params=pltpu.CompilerParams(vmem_limit_bytes=ADD_VMEM),
        name="pack",
    )(*(pltpu.with_memory_space_constraint(v, pltpu.HBM) for v in (activations, cotangent, relu_mask)))

    def swap(value, bit):
        return lax.ppermute(value, "chan", [(i, i ^ bit) for i in range(devices)])

    far = list(range(2, devices, 2))
    last = far.pop()
    early = [0, last]
    far.reverse()
    near = {bit: own if bit == 0 else swap(own, bit) for bit in early + far}

    weights = pl.pallas_call(
        load_kernel,
        out_shape=jax.ShapeDtypeStruct(weights.shape, weights.dtype),
        in_specs=[pl.BlockSpec(memory_space=pltpu.HBM), pl.BlockSpec(memory_space=pl.ANY)],
        out_specs=pl.BlockSpec(memory_space=pltpu.VMEM),
        scratch_shapes=[pltpu.SemaphoreType.DMA],
        compiler_params=pltpu.CompilerParams(vmem_limit_bytes=ADD_VMEM),
        name="load",
    )(pltpu.with_memory_space_constraint(weights, pltpu.HBM), own)

    me = lax.axis_index("chan")
    forward = lax.dynamic_slice_in_dim(weights, me * width, width, 3)
    backward = lax.dynamic_slice_in_dim(weights, me * width, width, 4)[::-1, ::-1, ::-1].swapaxes(3, 4)
    lhs = jnp.stack([forward, backward]).transpose(0, 1, 3, 4, 2, 5)
    lhs = lhs.reshape(2 * 9 * width, 3 * channels)
    column, start = [], 0
    for bits in (early, far):
        start = len(column)
        column += [
            (k, bit, i) for k in range(3) for near_bit in bits for bit in (near_bit, near_bit + 1) for i in range(width)
        ]
        column += [(3, 0, 0)] * (-len(column) % LANES)
    tap, bit, inside = (jnp.array(v, jnp.int32) for v in zip(*column))
    target = tap * channels + jnp.bitwise_xor(bit, me) * width + inside
    target = jnp.where(tap == 3, -1, target)
    order = (lax.broadcasted_iota(jnp.int32, (3 * channels, len(column)), 0) == target[None]).astype(jnp.bfloat16)
    lhs = jnp.dot(lhs, order, preferred_element_type=F32).astype(jnp.bfloat16).reshape(2, 9 * width, len(column))

    near[last], lhs = lax.optimization_barrier((near[last], lhs))
    blocks = {}
    for bit in early + far:
        blocks[bit] = near[bit]
        blocks[bit + 1] = swap(near[bit], 1)
    first = [blocks[bit + i] for bit in early for i in (0, 1)]
    second = [blocks[bit + i] for bit in far for i in (0, 1)]

    def call(kernel, out_shape, *args):
        return pl.pallas_call(
            kernel,
            out_shape=out_shape,
            in_specs=[pl.BlockSpec(memory_space=pltpu.VMEM)] * len(args),
            out_specs=jax.tree.map(lambda _: pl.BlockSpec(memory_space=pltpu.VMEM), out_shape),
            compiler_params=pltpu.CompilerParams(vmem_limit_bytes=CONV_VMEM),
            cost_estimate=pl.CostEstimate(flops=1 << 28, bytes_accessed=1 << 20, transcendentals=0),
        )(*args)

    def sums(*middle):
        return jax.ShapeDtypeStruct((2, rows, *middle, width, cols), F32)

    total = call(functools.partial(early_kernel, len(first)), sums(planes + 2), lhs, *first)
    largest = 9 * channels * INPUT_MAX * WEIGHT_MAX
    scale = 2.0 ** math.floor(math.log2(float(jnp.finfo(jnp.float16).max) / largest))

    def exchange(value, turn):
        partner = {}
        for i in range(turn, slabs - 1, ROUNDS):
            partner[i], partner[i + 1] = i + 1, i
        pairs = [
            (c * slabs + s, c * slabs + partner[s] if s in partner else (c ^ 1) * slabs + s)
            for c in range(devices)
            for s in range(slabs)
        ]
        value = (value * scale).astype(jnp.float16)
        value = lax.ppermute(value, ("chan", "slab"), pairs)
        return value.astype(F32) * (1 / scale)

    kernel = functools.partial(edge_kernel, len(second), start)
    sent, other = call(kernel, (sums(), sums()), lhs, total, *second)
    again, other = lax.optimization_barrier((sent, other))
    between = jnp.where(lax.rem(lax.axis_index("slab"), ROUNDS) == 2, again, other)
    edges = [exchange(value, turn) for turn, value in enumerate((sent, between, other))]
    inner = call(functools.partial(inner_kernel, len(second), start), sums(planes), lhs, total, *second)
    out = jax.ShapeDtypeStruct(activations.shape, jnp.bfloat16)
    return tuple(
        pl.pallas_call(
            add_kernel,
            out_shape=(out, out),
            in_specs=[pl.BlockSpec(memory_space=pltpu.VMEM)] * (ROUNDS + 1),
            out_specs=[pl.BlockSpec(memory_space=pltpu.VMEM)] * 2,
            scratch_shapes=[pltpu.VMEM((width * rows, cols), F32)],
            compiler_params=pltpu.CompilerParams(vmem_limit_bytes=ADD_VMEM),
            name="add",
        )(inner, *edges)
    )


def body(activations, cotangent, relu_mask, weights):
    width, planes, rows, cols = activations.shape
    devices = lax.axis_size("chan")
    aligned = (
        width % TILE == 0
        and cols == LANES
        and devices & (devices - 1) == 0
        and devices > 4
        and planes >= 2
        and rows % 8 == 0
        and lax.axis_size("slab") > 1
    )
    if not aligned:
        return general_body(activations, cotangent, relu_mask, weights)
    return aligned_body(activations, cotangent, relu_mask, weights)


def solution(mesh):
    placed = P("chan", "slab", None, None)
    return jax.shard_map(
        body,
        mesh=mesh,
        in_specs=(placed, placed, placed, P()),
        out_specs=(placed, placed),
        check_vma=False,
    )
```

```python
import functools
import math

import jax
import jax.numpy as jnp
from jax import lax
from jax.experimental import pallas as pl
from jax.experimental.pallas import tpu as pltpu
from jax.sharding import PartitionSpec as P


LANES = 128
TILE = 16
INPUT_MAX, WEIGHT_MAX = 6.0, 0.109375
CONV_VMEM, ADD_VMEM = 8 << 20, 4 << 20
F32 = jnp.float32
PIECES = 2
ROUNDS = 3


def with_halo(shard, sides, width):
    for axis, dim in sides:
        devices, length = (lax.axis_size(axis), shard.shape[dim])
        up = [(i, (i + 1) % devices) for i in range(devices - 1)]
        down = [(j, i) for i, j in up]
        last = lax.slice_in_dim(shard, length - width, length, axis=dim)
        first = lax.slice_in_dim(shard, 0, width, axis=dim)
        before = lax.ppermute(last, axis, up)
        after = lax.ppermute(first, axis, down)
        shard = jnp.concatenate([before, shard, after], axis=dim)
    return shard


def tap_sum(weights, padded, planes, height, breadth, equation, flipped):
    total = None
    for i in range(3):
        for j in range(3):
            for k in range(3):
                a, b, c = (2 - i, 2 - j, 2 - k) if flipped else (i, j, k)
                window = padded[:, a : a + planes, b : b + height, c : c + breadth]
                term = jnp.einsum(equation, weights[i, j, k], window, preferred_element_type=F32)
                total = term if total is None else total + term
    return total.astype(jnp.bfloat16)


def general_body(activations, cotangent, relu_mask, weights):
    planes, breadth = activations.shape[1], activations.shape[3]
    masked = jnp.where(relu_mask == 1, cotangent, jnp.zeros_like(cotangent))
    stacked = jnp.stack([activations, masked])
    patches = lax.all_to_all(stacked, "chan", split_axis=3, concat_axis=1, tiled=True)
    rimmed = with_halo(patches, (("chan", 3), ("slab", 2)), 1)
    padded = jnp.pad(rimmed, ((0, 0), (0, 0), (0, 0), (0, 0), (1, 1)))
    height = patches.shape[3]
    pre = tap_sum(weights, padded[0], planes, height, breadth, "oi,idhw->odhw", False)
    grad = tap_sum(weights, padded[1], planes, height, breadth, "oi,odhw->idhw", True)
    return tuple(
        lax.all_to_all(block, "chan", split_axis=0, concat_axis=2, tiled=True) for block in (pre, grad)
    )


def window(blocks, a, places, height=3):
    sides = []
    for r, p in places:
        pieces = []
        for row in range(r - 1, r - 1 + height):
            inside = 0 <= row < blocks[0].shape[1]
            pieces += [b[a, row, p] if inside else jnp.zeros(b.shape[3:], b.dtype) for b in blocks]
        sides.append(jnp.concatenate(pieces, axis=0))
    return jnp.concatenate(sides, axis=1)


def columns(taps):
    left, mid, right = taps
    lane = lax.broadcasted_iota(jnp.int32, mid.shape, 1)
    left = jnp.where(lane == 0, 0.0, pltpu.roll(left, 1, 1))
    right = jnp.where(lane == mid.shape[1] - 1, 0.0, pltpu.roll(right, mid.shape[1] - 1, 1))
    return left + mid + right


def all_planes(lhs, blocks, a, r, wanted):
    _, _, planes, width, cols = blocks[0].shape
    y = jnp.dot(lhs, window(blocks, a, [(r, p) for p in range(planes)]), preferred_element_type=F32)

    def part(t, k, p):
        top = (t * 3 + k) * width
        return y[top : top + width, p * cols : (p + 1) * cols]

    def plane(q):
        inputs = [p for p in range(planes) if 0 <= p - q + 1 <= 2]
        return columns([functools.reduce(jnp.add, [part(p - q + 1, k, p) for p in inputs]) for k in range(3)])

    return [plane(q) for q in wanted]


def pack_kernel(act_hbm, cot_hbm, mask_hbm, own_ref, act_ref, cot_ref, mask_ref, turned_ref, sems):
    width, planes, rows, cols = act_ref.shape
    pairs = ((act_hbm, act_ref), (cot_hbm, cot_ref), (mask_hbm, mask_ref))
    step = width // PIECES
    copies = [
        [
            pltpu.make_async_copy(source.at[pl.ds(k * step, step)], target.at[pl.ds(k * step, step)], sems.at[i, k])
            for k in range(PIECES)
        ]
        for i, (source, target) in enumerate(pairs)
    ]
    for i in (2, 0, 1):
        for k in range(PIECES):
            copies[i][k].start()

    def turn(a):
        for p in range(planes):
            value = (act_ref, cot_ref)[a][:, p].astype(F32)
            if a == 1:
                value = jnp.where(mask_ref[:, p] == 1, value, 0.0)
            turned_ref[a, p] = value.reshape(width * rows, cols)
            for r in range(rows):
                own_ref[a, r, p] = turned_ref[a, p, pl.ds(r, width, stride=rows), :].astype(jnp.bfloat16)

    for copy in copies[0]:
        copy.wait()
    turn(0)
    for copy in copies[1] + copies[2]:
        copy.wait()
    turn(1)


def load_kernel(weights_hbm, own_ref, weights_ref, sem):
    copy = pltpu.make_async_copy(weights_hbm, weights_ref, sem)
    copy.start()
    copy.wait()


def early_kernel(count, lhs_ref, *refs):
    blocks, sum_ref = refs[:count], refs[count]
    arrays, rows, planes, width, _ = blocks[0].shape
    depth = 3 * count * width
    for a in range(arrays):
        lhs = lhs_ref[a, :, :depth]
        for r in range(rows):
            for q, value in enumerate(all_planes(lhs, blocks, a, r, range(-1, planes + 1))):
                sum_ref[a, r, q] = value


def edge_kernel(count, first, lhs_ref, sum_ref, *refs):
    blocks, edge_ref = refs[:count], refs[count]
    arrays, rows, planes, width, cols = blocks[0].shape
    height = 3 * width
    above = (lax.rem(lax.axis_index("slab"), ROUNDS) == 0) == first
    p, q = jnp.where(above, planes - 1, 0), jnp.where(above, planes + 1, 0)
    top = pl.multiple_of(jnp.where(above, 0, 2 * height), TILE)
    for a in range(arrays):
        lhs = jnp.concatenate([lhs_ref[a, i, pl.ds(top, height)] for i in range(2)], axis=0)
        for r in range(0, rows, 4):
            y = jnp.dot(lhs, window(blocks, a, [(r, p), (r + 2, p)], 4), preferred_element_type=F32)
            for i in range(4):
                side, low = y[:, i // 2 * cols : (i // 2 + 1) * cols], i % 2 * height
                taps = [side[low + k * width : low + (k + 1) * width] for k in range(3)]
                edge_ref[a, r + i] = columns(taps) + sum_ref[a, r + i, q]


def inner_kernel(count, start, lhs_ref, sum_ref, *refs):
    blocks, inner_ref = refs[:count], refs[count]
    arrays, rows, planes, width, _ = blocks[0].shape
    depth = 3 * count * width
    for a in range(arrays):
        lhs = lhs_ref[a, :, start : start + depth]
        for r in range(rows):
            for p, value in enumerate(all_planes(lhs, blocks, a, r, range(planes))):
                inner_ref[a, r, p] = value + sum_ref[a, r, p + 1]


def add_kernel(inner_ref, *refs):
    edge_refs, (pre_ref, grad_ref, turned_ref) = refs[:ROUNDS], refs[ROUNDS:]
    _, rows, planes, width, cols = inner_ref.shape
    slab = lax.axis_index("slab")
    below, above = slab > 0, slab < lax.axis_size("slab") - 1

    def received(a, r, pair, exists):
        value = edge_refs[0][a, r]
        for j in range(1, ROUNDS):
            value = jnp.where(lax.rem(pair, ROUNDS) == j, edge_refs[j][a, r], value)
        return jnp.where(exists, value, 0.0)

    for a, out_ref in enumerate((pre_ref, grad_ref)):
        for p in range(planes):
            for r in range(rows):
                value = inner_ref[a, r, p]
                if p == 0:
                    value = value + received(a, r, slab + ROUNDS - 1, below)
                if p == planes - 1:
                    value = value + received(a, r, slab, above)
                turned_ref[pl.ds(r, width, stride=rows), :] = value
            out_ref[:, p] = turned_ref[...].reshape(width, rows, cols).astype(jnp.bfloat16)


def aligned_body(activations, cotangent, relu_mask, weights):
    width, planes, rows, cols = activations.shape
    devices, slabs = lax.axis_size("chan"), lax.axis_size("slab")
    channels = width * devices
    own = pl.pallas_call(
        pack_kernel,
        out_shape=jax.ShapeDtypeStruct((2, rows, planes, width, cols), jnp.bfloat16),
        in_specs=[pl.BlockSpec(memory_space=pltpu.HBM)] * 3,
        out_specs=pl.BlockSpec(memory_space=pltpu.VMEM),
        scratch_shapes=[pltpu.VMEM(v.shape, v.dtype) for v in (activations, cotangent, relu_mask)]
        + [pltpu.VMEM((2, planes, width * rows, cols), F32), pltpu.SemaphoreType.DMA((3, PIECES))],
        compiler_params=pltpu.CompilerParams(vmem_limit_bytes=ADD_VMEM),
        name="pack",
    )(*(pltpu.with_memory_space_constraint(v, pltpu.HBM) for v in (activations, cotangent, relu_mask)))

    def swap(value, bit):
        return lax.ppermute(value, "chan", [(i, i ^ bit) for i in range(devices)])

    far = list(range(2, devices, 2))
    last = far.pop()
    early = [0, last]
    far.reverse()
    near = {bit: own if bit == 0 else swap(own, bit) for bit in early + far}

    weights = pl.pallas_call(
        load_kernel,
        out_shape=jax.ShapeDtypeStruct(weights.shape, weights.dtype),
        in_specs=[pl.BlockSpec(memory_space=pltpu.HBM), pl.BlockSpec(memory_space=pl.ANY)],
        out_specs=pl.BlockSpec(memory_space=pltpu.VMEM),
        scratch_shapes=[pltpu.SemaphoreType.DMA],
        compiler_params=pltpu.CompilerParams(vmem_limit_bytes=ADD_VMEM),
        name="load",
    )(pltpu.with_memory_space_constraint(weights, pltpu.HBM), own)

    me = lax.axis_index("chan")
    forward = lax.dynamic_slice_in_dim(weights, me * width, width, 3)
    backward = lax.dynamic_slice_in_dim(weights, me * width, width, 4)[::-1, ::-1, ::-1].swapaxes(3, 4)
    lhs = jnp.stack([forward, backward]).transpose(0, 1, 3, 4, 2, 5)
    lhs = lhs.reshape(2 * 9 * width, 3 * channels)
    column, start = [], 0
    for bits in (early, far):
        start = len(column)
        column += [
            (k, bit, i) for k in range(3) for near_bit in bits for bit in (near_bit, near_bit + 1) for i in range(width)
        ]
        column += [(3, 0, 0)] * (-len(column) % LANES)
    tap, bit, inside = (jnp.array(v, jnp.int32) for v in zip(*column))
    target = tap * channels + jnp.bitwise_xor(bit, me) * width + inside
    target = jnp.where(tap == 3, -1, target)
    order = (lax.broadcasted_iota(jnp.int32, (3 * channels, len(column)), 0) == target[None]).astype(jnp.bfloat16)
    lhs = jnp.dot(lhs, order, preferred_element_type=F32).astype(jnp.bfloat16).reshape(2, 9 * width, len(column))
    block = 2 * len(far) * width
    pair = jnp.stack([jnp.pad(lhs[:, :, start : start + 3 * block], ((0, 0), (0, 0), (i * block, block - i * block))) for i in range(2)], axis=1)

    near[last], lhs, pair = lax.optimization_barrier((near[last], lhs, pair))
    blocks = {}
    for bit in early + far:
        blocks[bit] = near[bit]
        blocks[bit + 1] = swap(near[bit], 1)
    first = [blocks[bit + i] for bit in early for i in (0, 1)]
    second = [blocks[bit + i] for bit in far for i in (0, 1)]

    def call(kernel, out_shape, *args):
        return pl.pallas_call(
            kernel,
            out_shape=out_shape,
            in_specs=[pl.BlockSpec(memory_space=pltpu.VMEM)] * len(args),
            out_specs=jax.tree.map(lambda _: pl.BlockSpec(memory_space=pltpu.VMEM), out_shape),
            compiler_params=pltpu.CompilerParams(vmem_limit_bytes=CONV_VMEM),
            cost_estimate=pl.CostEstimate(flops=1 << 28, bytes_accessed=1 << 20, transcendentals=0),
        )(*args)

    def sums(*middle):
        return jax.ShapeDtypeStruct((2, rows, *middle, width, cols), F32)

    total = call(functools.partial(early_kernel, len(first)), sums(planes + 2), lhs, *first)
    largest = 9 * channels * INPUT_MAX * WEIGHT_MAX
    scale = 2.0 ** math.floor(math.log2(float(jnp.finfo(jnp.float16).max) / largest))

    def exchange(value, turn):
        partner = {}
        for i in range(turn, slabs - 1, ROUNDS):
            partner[i], partner[i + 1] = i + 1, i
        pairs = [
            (c * slabs + s, c * slabs + partner[s] if s in partner else (c ^ 1) * slabs + s)
            for c in range(devices)
            for s in range(slabs)
        ]
        value = (value * scale).astype(jnp.float16)
        value = lax.ppermute(value, ("chan", "slab"), pairs)
        return value.astype(F32) * (1 / scale)

    sent, other = (
        call(functools.partial(edge_kernel, len(second), i == 0), sums(), pair, total, *second)
        for i in range(2)
    )
    again, other = lax.optimization_barrier((sent, other))
    between = jnp.where(lax.rem(lax.axis_index("slab"), ROUNDS) == 2, again, other)
    edges = [exchange(value, turn) for turn, value in enumerate((sent, between, other))]
    inner = call(functools.partial(inner_kernel, len(second), start), sums(planes), lhs, total, *second)
    out = jax.ShapeDtypeStruct(activations.shape, jnp.bfloat16)
    return tuple(
        pl.pallas_call(
            add_kernel,
            out_shape=(out, out),
            in_specs=[pl.BlockSpec(memory_space=pltpu.VMEM)] * (ROUNDS + 1),
            out_specs=[pl.BlockSpec(memory_space=pltpu.VMEM)] * 2,
            scratch_shapes=[pltpu.VMEM((width * rows, cols), F32)],
            compiler_params=pltpu.CompilerParams(
                vmem_limit_bytes=ADD_VMEM, allow_input_fusion=[False] + [True] * ROUNDS
            ),
            name="add",
        )(inner, *edges)
    )


def body(activations, cotangent, relu_mask, weights):
    width, planes, rows, cols = activations.shape
    devices = lax.axis_size("chan")
    aligned = (
        width % TILE == 0
        and cols == LANES
        and devices & (devices - 1) == 0
        and devices > 4
        and planes >= 2
        and rows % 8 == 0
        and lax.axis_size("slab") > 1
    )
    if not aligned:
        return general_body(activations, cotangent, relu_mask, weights)
    return aligned_body(activations, cotangent, relu_mask, weights)


def solution(mesh):
    placed = P("chan", "slab", None, None)
    return jax.shard_map(
        body,
        mesh=mesh,
        in_specs=(placed, placed, placed, P()),
        out_specs=(placed, placed),
        check_vma=False,
    )
```
